128 devices in a mesh: row: 16 (over y, z_lo, core), col: 8 (over x, z_hi).
Axes of the slice: x: 4, y: 4, z: 4 (z_hi: 2, z_lo: 2; z = z_hi * 2 + z_lo), core: 2. Of those that a mesh axis runs over, the one named last changes fastest.
Arguments:
- record: bfloat16 [6, 2048, 2560], P(None, ('row', 'col')), may hold values from -6 to 6
- taps: float32 [200], replicated, may hold values from -0.4375 to 0.4375
- plan: int32 [6], replicated, may hold values from 0 to 5, each once
- quality: int32 [2048], P(('row', 'col')), may hold values 0 or 1
Outputs:
- correlation: float32 [51, 2048, 2048], P(None, 'row', 'col')
The draws below stay inside these ranges and needn't reach their ends.
Inputs may be any that keep to these rules, and one draw needn't show every extreme that they name: plan is a permutation of the recorded sub-windows; its first 4 entries name the ones that are stacked.
All inputs are finite; a program needn't handle non-finite values. No bound on the sum of `quality` on one device may be relied on, other than what follows from the above.
Results may differ from the reference program's by a relative error of at most 0.0039.
Values may be sent and summed in bfloat16 or wider, within the bound.
No kernel may reach another device: no remote copies, remote signals or barrier semaphores. Data moves between devices by JAX's collectives and lax.ppermute only.
A program may use at most 64 MiB of HBM per device.

```python
import math
import jax
import jax.numpy as jnp
from jax import lax

C = 2048
STRIDE = 20
TAPS = 200
HALFWIN = 32
MAXLAG = 25
SUB = 4
SLOTS = 6
RAW = 2560
LAGS = 51


def place_ends(array, key, least, high):
    longest = array.shape.index(max(array.shape))
    spots = []
    for shift in (0, 1):
        where = [jax.random.randint(jax.random.fold_in(key, axis), (), 0, length) for axis, length in enumerate(array.shape)]
        where[longest] = (where[longest] + shift) % array.shape[longest]
        spots.append(tuple(where))
    return array.at[spots[0]].set(least).at[spots[1]].set(high)


def shard_levels(key, shape, shards, smallest, high):
    gain = 1.0
    for position, parts in shards:
        steps = jax.random.uniform(jax.random.fold_in(jax.random.fold_in(key, 6), position), (parts,), jnp.float32, smallest / len(shards), high / len(shards))
        gain = gain * jnp.repeat(jnp.exp(steps), shape[position] // parts).reshape((-1,) + (1,) * (len(shape) - 1 - position))
    return gain


def gaussian(stream_key, extent, deviation, bound, pieces=(), held_as=jnp.bfloat16):
    drawn = jax.random.normal(stream_key, extent, jnp.float32) * deviation
    if len(pieces) > 0:
        drawn = shard_levels(stream_key, extent, pieces, -0.22, 0.18) * drawn
    return jnp.clip(drawn, min=-bound, max=bound).astype(held_as)


def setup_inputs(seed: int = 0) -> dict:
    arg_keys = jax.random.split(jax.random.key(seed), 5)
    return {
        "record": gaussian(arg_keys[0], (SLOTS, C, RAW), 1.0, 6.0, ((1, 128),)),
        "taps": gaussian(arg_keys[1], (TAPS,), TAPS ** -0.5, 0.4375, (), jnp.float32),
        "plan": jax.random.permutation(arg_keys[2], SLOTS).astype(jnp.int32),
        "quality": place_ends((jax.random.randint(arg_keys[3], (C,), 0, 8) < 7).astype(jnp.int32), jax.random.fold_in(arg_keys[3], 1), 0, 1),
    }


def decimate(picked, taps):
    window_count, chan_count, raw_length = picked.shape
    frame_count = raw_length // STRIDE
    block_count = TAPS // STRIDE
    blocks = picked.astype(jnp.float32).reshape(window_count, chan_count, frame_count, STRIDE)
    blocks = jnp.pad(blocks, ((0, 0), (0, 0), (0, block_count - 1), (0, 0)))
    tap_table = taps.reshape(block_count, STRIDE)
    filtered = jnp.zeros((chan_count, window_count, frame_count), jnp.float32)
    for offset in range(block_count):
        filtered = filtered + jnp.einsum('sckr,r->csk', blocks[:, :, offset:offset + frame_count, :], tap_table[offset], precision=lax.Precision.HIGHEST)
    return filtered

def whiten(decimated, quality):
    frame_count = decimated.shape[2]
    places = jnp.arange(frame_count, dtype=jnp.int32)
    band_matrix = (jnp.abs(places[:, None] - places[None, :]) <= HALFWIN).astype(jnp.float32)
    envelope = jnp.einsum('csk,kj->csj', jnp.abs(decimated), band_matrix, precision=lax.Precision.HIGHEST) / (2 * HALFWIN + 1)
    scaled = decimated / (envelope + 1e-05) * quality.astype(jnp.float32)[:, None, None]
    return scaled.astype(jnp.bfloat16)

def correlate(source, receiver):
    source_count, window_count, frame_count = source.shape
    receiver_count = receiver.shape[0]
    flat_source = source.astype(jnp.float32).reshape(source_count, window_count * frame_count)
    padded = jnp.pad(receiver.astype(jnp.float32), ((0, 0), (0, 0), (MAXLAG, MAXLAG)))

    def one_lag(offset):
        moved = lax.dynamic_slice_in_dim(padded, offset, frame_count, 2).reshape(receiver_count, window_count * frame_count)
        return lax.dot_general(flat_source, moved, (((1,), (1,)), ((), ())), precision=lax.Precision.HIGHEST, preferred_element_type=jnp.float32)
    stacked = lax.map(one_lag, jnp.arange(LAGS, dtype=jnp.int32))
    return stacked * (1.0 / math.sqrt(window_count * frame_count))

def reference(record, taps, plan, quality):
    picked = jnp.take(record, plan[:SUB], axis=0)
    whitened = whiten(decimate(picked, taps), quality)
    return correlate(whitened, whitened)
```

```python
import math

import jax
import jax.numpy as jnp
from jax import lax
from jax.experimental import pallas as pl
from jax.experimental.pallas import tpu as pltpu
from jax.sharding import PartitionSpec as P

STRIDE = 20
TAPS = 200
HALFWIN = 32
MAXLAG = 25
SUB = 4
LAGS = 51
FRAMES = 128
SEGMENT = 32 * STRIDE
SPAN = 896
AXES = ("row", "col")
GROUP = 3


def whiten_kernel(plan_ref, w0, w1, w2, w3, taps_ref, quality_ref, out_ref):
    chans = out_ref.shape[0]
    f32, bf16 = jnp.float32, jnp.bfloat16
    taps = taps_ref[...].reshape(1, TAPS)
    table = jnp.broadcast_to(
        jnp.concatenate([taps, jnp.zeros((1, SPAN - TAPS), f32)], axis=1), (32, SPAN)
    )
    k = lax.broadcasted_iota(jnp.int32, (32, SPAN), 0)
    for bit in range(5):
        moved = pltpu.roll(table, STRIDE << bit, 1)
        table = jnp.where((k >> bit) & 1 == 1, moved, table)
    high = table.astype(bf16)
    low = (table - high.astype(f32)).astype(bf16)
    filters = jnp.concatenate([high] * 4 + [low] * 4, axis=0)
    zeros = jnp.zeros((chans, SPAN - SEGMENT), bf16)
    pieces = []
    for window in (w0, w1, w2, w3):
        samples = jnp.concatenate([window[0], zeros], axis=1)
        for b in range(4):
            pieces.append(samples[:, b * SEGMENT : b * SEGMENT + SPAN])
    both = lax.dot_general(
        jnp.concatenate(pieces, axis=0),
        filters,
        (((1,), (1,)), ((), ())),
        preferred_element_type=f32,
    )
    both = both[:, :FRAMES] + both[:, FRAMES:]
    lane = lax.broadcasted_iota(jnp.int32, (chans, FRAMES), 1)
    rows = []
    for s in range(SUB):
        p = [both[(s * 4 + b) * chans : (s * 4 + b + 1) * chans] for b in range(4)]
        rows.append(
            jnp.where(
                lane < 64,
                jnp.where(lane < 32, p[0], p[1]),
                jnp.where(lane < 96, p[2], p[3]),
            )
        )
    decimated = jnp.concatenate(rows, axis=0)
    size = jnp.abs(decimated)
    size_high = size.astype(bf16)
    size_low = (size - size_high.astype(f32)).astype(bf16)
    i = lax.broadcasted_iota(jnp.int32, (2 * FRAMES, FRAMES), 0) & (FRAMES - 1)
    j = lax.broadcasted_iota(jnp.int32, (2 * FRAMES, FRAMES), 1)
    band = jnp.where(jnp.abs(i - j) <= HALFWIN, 1.0, 0.0).astype(bf16)
    envelope = jnp.dot(
        jnp.concatenate([size_high, size_low], axis=1), band, preferred_element_type=f32
    ) * (1.0 / (2 * HALFWIN + 1))
    a = lax.broadcasted_iota(jnp.int32, (chans, chans), 0)
    b = lax.broadcasted_iota(jnp.int32, (chans, chans), 1)
    across = jnp.broadcast_to(
        quality_ref[...].reshape(1, chans).astype(f32), (chans, chans)
    )
    quality = jnp.sum(jnp.where(a == b, across, 0.0), axis=1, keepdims=True)
    for s in range(SUB):
        d = decimated[s * chans : (s + 1) * chans]
        e = envelope[s * chans : (s + 1) * chans]
        out_ref[:, s * FRAMES : (s + 1) * FRAMES] = (d / (e + 1e-05) * quality).astype(bf16)


def whiten(record, taps, plan, quality):
    chans, raw = record.shape[1:]

    def window(s):
        return pl.BlockSpec((1, chans, raw), lambda i, plan: (plan[s], 0, 0))

    return pl.pallas_call(
        whiten_kernel,
        name="whiten",
        out_shape=jax.ShapeDtypeStruct((chans, SUB * FRAMES), jnp.bfloat16),
        grid_spec=pltpu.PrefetchScalarGridSpec(
            num_scalar_prefetch=1,
            grid=(1,),
            in_specs=[window(s) for s in range(SUB)]
            + [
                pl.BlockSpec(taps.shape, lambda i, plan: (0,)),
                pl.BlockSpec(quality.shape, lambda i, plan: (0,)),
            ],
            out_specs=pl.BlockSpec((chans, SUB * FRAMES), lambda i, plan: (0, 0)),
        ),
        cost_estimate=pl.CostEstimate(flops=1 << 28, bytes_accessed=1 << 19, transcendentals=0),
    )(plan, record, record, record, record, taps, quality)


def row_slot(row):
    return ((row & 1) << 3) | ((row >> 1) ^ 4)


S_MASKS = (1, 4, 2)
R_MASKS = (8, 4, 2, 1)
R_SLOTS = (4, 2, 1, 8)


def correlate_kernel(s_ref, r_ref, out_ref, source, receiver, products, sems):
    count, length = source.shape
    chans = count // 8
    col = lax.axis_index("col")
    slot = row_slot(lax.axis_index("row"))
    for t in range(8):
        place = col
        for bit, mask in enumerate(S_MASKS):
            place = place ^ (mask if t >> bit & 1 else 0)
        source[pl.ds(pl.multiple_of(place * chans, chans), chans)] = s_ref[
            t * chans : (t + 1) * chans
        ].astype(jnp.float32)
    ordered = []
    for t in range(16):
        place = slot
        for bit, mask in enumerate(R_SLOTS):
            place = place ^ (mask if t >> bit & 1 else 0)
        receiver[pl.ds(pl.multiple_of(place * chans, chans), chans)] = r_ref[
            t * chans : (t + 1) * chans
        ]
    turned = receiver[...].T
    lane = lax.broadcasted_iota(jnp.int32, (count, FRAMES), 1)
    scale = 1.0 / math.sqrt(length)

    def copy(g):
        part = pl.ds(g * GROUP, GROUP)
        return pltpu.make_async_copy(products.at[part], out_ref.at[part], sems.at[g])

    for g in range(LAGS // GROUP):
        moved = []
        for q in range(g * GROUP, (g + 1) * GROUP):
            shift = q - MAXLAG
            inside = (lane >= shift) & (lane < shift + FRAMES)
            moved.append(
                jnp.concatenate(
                    [
                        jnp.where(
                            inside,
                            pltpu.roll(
                                source[:, s * FRAMES : (s + 1) * FRAMES], shift % FRAMES, 1
                            ),
                            0.0,
                        ).astype(jnp.bfloat16)
                        for s in range(SUB)
                    ],
                    axis=1,
                )
            )
        product = jnp.dot(
            jnp.concatenate(moved, axis=0), turned, preferred_element_type=jnp.float32
        )
        products[g * GROUP : (g + 1) * GROUP] = (product * scale).reshape(GROUP, count, -1)
        copy(g).start()
    for g in range(LAGS // GROUP):
        copy(g).wait()


def correlate(source, receiver):
    count, width = source.shape[0], receiver.shape[0]
    whole = pl.BlockSpec(memory_space=pltpu.VMEM)
    return pl.pallas_call(
        correlate_kernel,
        name="correlate",
        out_shape=jax.ShapeDtypeStruct((LAGS, count, width), jnp.float32),
        in_specs=[whole, whole],
        out_specs=pl.BlockSpec(memory_space=pl.ANY),
        scratch_shapes=[
            pltpu.VMEM(source.shape, jnp.float32),
            pltpu.VMEM(receiver.shape, jnp.bfloat16),
            pltpu.VMEM((LAGS, count, width), jnp.float32),
            pltpu.SemaphoreType.DMA((LAGS // GROUP,)),
        ],
        cost_estimate=pl.CostEstimate(flops=1 << 31, bytes_accessed=1 << 23, transcendentals=0),
    )(source, receiver)


def send(block, target):
    pairs = [
        (row * 8 + col, target(row, col)[0] * 8 + target(row, col)[1])
        for row in range(16)
        for col in range(8)
    ]
    return lax.ppermute(block, AXES, pairs)


def to_column(row, col):
    y, z_lo, core = row >> 2, row >> 1 & 1, row & 1
    x, z_hi = col >> 1, col & 1
    return (x ^ 2) * 4 + z_hi * 2 + core, y * 2 + z_lo


def body(record, taps, plan, quality):
    whitened = whiten(record, taps, plan, quality)
    source = whitened
    for mask in S_MASKS:
        other = send(source, lambda row, col: (row, col ^ mask))
        source = jnp.concatenate([source, other], axis=0)
    receiver = send(whitened, to_column)
    for mask in R_MASKS:
        other = send(receiver, lambda row, col: (row ^ mask, col))
        receiver = jnp.concatenate([receiver, other], axis=0)
    return correlate(source, receiver)


def solution(mesh):
    in_specs = (P(None, AXES, None), P(), P(), P(AXES))
    out_specs = P(None, "row", "col")
    return jax.shard_map(body, mesh=mesh, in_specs=in_specs, out_specs=out_specs, check_vma=False)
```

```python
import math

import jax
import jax.numpy as jnp
from jax import lax
from jax.experimental import pallas as pl
from jax.experimental.pallas import tpu as pltpu
from jax.sharding import PartitionSpec as P


STRIDE = 20
TAPS = 200
HALFWIN = 32
MAXLAG = 25
SUB = 4
LAGS = 51
FRAMES = 128
SEGMENT = 32 * STRIDE
SPAN = 896
AXES = ("row", "col")
GROUP = 3


def whiten_kernel(plan_ref, record_ref, taps_ref, quality_ref, out_ref, samples, sems):
    chans = out_ref.shape[0]
    f32, bf16 = jnp.float32, jnp.bfloat16
    raw = record_ref.shape[2]

    def copy(s):
        return pltpu.make_async_copy(
            record_ref.at[plan_ref[s]], samples.at[s, :, pl.ds(0, raw)], sems.at[s]
        )

    for s in range(SUB):
        copy(s).start()
    samples[:, :, raw:] = jnp.zeros((SUB, chans, samples.shape[2] - raw), bf16)
    taps = taps_ref[...].reshape(1, TAPS)
    table = jnp.broadcast_to(
        jnp.concatenate([taps, jnp.zeros((1, SPAN - TAPS), f32)], axis=1), (32, SPAN)
    )
    k = lax.broadcasted_iota(jnp.int32, (32, SPAN), 0)
    for bit in range(5):
        moved = pltpu.roll(table, STRIDE << bit, 1)
        table = jnp.where((k >> bit) & 1 == 1, moved, table)
    high = table.astype(bf16)
    low = (table - high.astype(f32)).astype(bf16)
    filters = jnp.concatenate([high] * 4 + [low] * 4, axis=0)
    i = lax.broadcasted_iota(jnp.int32, (2 * FRAMES, FRAMES), 0) & (FRAMES - 1)
    j = lax.broadcasted_iota(jnp.int32, (2 * FRAMES, FRAMES), 1)
    band = jnp.where(jnp.abs(i - j) <= HALFWIN, 1.0, 0.0).astype(bf16)
    a = lax.broadcasted_iota(jnp.int32, (chans, chans), 0)
    b = lax.broadcasted_iota(jnp.int32, (chans, chans), 1)
    across = jnp.broadcast_to(
        quality_ref[...].reshape(1, chans).astype(f32), (chans, chans)
    )
    quality = jnp.sum(jnp.where(a == b, across, 0.0), axis=1, keepdims=True)
    for s in range(SUB):
        copy(s).wait()
    both = lax.dot_general(
        jnp.concatenate(
            [
                samples[s, :, b * SEGMENT : b * SEGMENT + SPAN]
                for s in range(SUB)
                for b in range(4)
            ],
            axis=0,
        ),
        filters,
        (((1,), (1,)), ((), ())),
        preferred_element_type=f32,
    )
    both = both[:, :FRAMES] + both[:, FRAMES:]
    lane = lax.broadcasted_iota(jnp.int32, (chans, FRAMES), 1)
    rows = []
    for s in range(SUB):
        p = [both[(s * 4 + b) * chans : (s * 4 + b + 1) * chans] for b in range(4)]
        rows.append(
            jnp.where(
                lane < 64,
                jnp.where(lane < 32, p[0], p[1]),
                jnp.where(lane < 96, p[2], p[3]),
            )
        )
    decimated = jnp.concatenate(rows, axis=0)
    size = jnp.abs(decimated)
    size_high = size.astype(bf16)
    size_low = (size - size_high.astype(f32)).astype(bf16)
    envelope = jnp.dot(
        jnp.concatenate([size_high, size_low], axis=1), band, preferred_element_type=f32
    ) * (1.0 / (2 * HALFWIN + 1))
    for s in range(SUB):
        d = decimated[s * chans : (s + 1) * chans]
        e = envelope[s * chans : (s + 1) * chans]
        out_ref[:, s * FRAMES : (s + 1) * FRAMES] = (d / (e + 1e-05) * quality).astype(bf16)


def whiten(record, taps, plan, quality):
    chans, raw = record.shape[1:]
    return pl.pallas_call(
        whiten_kernel,
        name="whiten",
        out_shape=jax.ShapeDtypeStruct((chans, SUB * FRAMES), jnp.bfloat16),
        in_specs=[
            pl.BlockSpec(memory_space=pltpu.SMEM),
            pl.BlockSpec(memory_space=pltpu.HBM),
            pl.BlockSpec(memory_space=pltpu.VMEM),
            pl.BlockSpec(memory_space=pltpu.VMEM),
        ],
        out_specs=pl.BlockSpec(memory_space=pltpu.VMEM),
        scratch_shapes=[
            pltpu.VMEM((SUB, chans, raw + SPAN - SEGMENT), jnp.bfloat16),
            pltpu.SemaphoreType.DMA((SUB,)),
        ],
        compiler_params=pltpu.CompilerParams(vmem_limit_bytes=8 << 20),
        cost_estimate=pl.CostEstimate(flops=1 << 28, bytes_accessed=1 << 19, transcendentals=0),
    )(*(pltpu.with_memory_space_constraint(v, pltpu.HBM) for v in (plan, record, taps, quality)))


S_MASKS = (1, 4, 2)


def spread(index, *masks):
    place = 0
    for bit, mask in enumerate(masks):
        if index >> bit & 1:
            place = place ^ mask
    return place


def correlate_kernel(s0_ref, s1_ref, r0_ref, r1_ref, out_ref, source, receiver, products, sems):
    count, length = source.shape
    chans = count // 8
    col, row = lax.axis_index("col"), lax.axis_index("row")
    for t in range(8):
        place = col ^ spread(t, *S_MASKS)
        part = (s0_ref, s1_ref)[t // 4]
        source[pl.ds(pl.multiple_of(place * chans, chans), chans)] = part[
            t % 4 * chans : (t % 4 + 1) * chans
        ].astype(jnp.float32)
    for half in range(2):
        core = (row & 1) ^ half
        part = (r0_ref, r1_ref)[half]
        for t in range(4):
            place = (row >> 1) ^ (4 - 2 * core) ^ spread(t, 2 - core, 1 + core)
            for j in range(2):
                start = ((core ^ j) * 8 + place) * chans
                receiver[pl.ds(pl.multiple_of(start, chans), chans)] = part[
                    (t * 2 + j) * chans : (t * 2 + j + 1) * chans
                ]
    turned = receiver[...].T
    lane = lax.broadcasted_iota(jnp.int32, (count, FRAMES), 1)
    scale = 1.0 / math.sqrt(length)

    def copy(g):
        part = pl.ds(g * GROUP, GROUP)
        return pltpu.make_async_copy(products.at[part], out_ref.at[part], sems.at[g])

    for g in range(LAGS // GROUP):
        moved = []
        for q in range(g * GROUP, (g + 1) * GROUP):
            shift = q - MAXLAG
            inside = (lane >= shift) & (lane < shift + FRAMES)
            moved.append(
                jnp.concatenate(
                    [
                        jnp.where(
                            inside,
                            pltpu.roll(
                                source[:, s * FRAMES : (s + 1) * FRAMES], shift % FRAMES, 1
                            ),
                            0.0,
                        ).astype(jnp.bfloat16)
                        for s in range(SUB)
                    ],
                    axis=1,
                )
            )
        product = jnp.dot(
            jnp.concatenate(moved, axis=0), turned, preferred_element_type=jnp.float32
        )
        products[g * GROUP : (g + 1) * GROUP] = (product * scale).reshape(GROUP, count, -1)
        copy(g).start()
    for g in range(LAGS // GROUP):
        copy(g).wait()


def correlate(*parts):
    count, width = 2 * parts[0].shape[0], 2 * parts[2].shape[0]
    length = parts[0].shape[1]
    whole = pl.BlockSpec(memory_space=pltpu.VMEM)
    return pl.pallas_call(
        correlate_kernel,
        name="correlate",
        out_shape=jax.ShapeDtypeStruct((LAGS, count, width), jnp.float32),
        in_specs=[whole] * 4,
        out_specs=pl.BlockSpec(memory_space=pl.ANY),
        scratch_shapes=[
            pltpu.VMEM((count, length), jnp.float32),
            pltpu.VMEM((width, length), jnp.bfloat16),
            pltpu.VMEM((LAGS, count, width), jnp.float32),
            pltpu.SemaphoreType.DMA((LAGS // GROUP,)),
        ],
        compiler_params=pltpu.CompilerParams(vmem_limit_bytes=24 << 20),
        cost_estimate=pl.CostEstimate(flops=1 << 31, bytes_accessed=1 << 23, transcendentals=0),
    )(*parts)


def send(block, target):
    pairs = [
        (row * 8 + col, target(row, col)[0] * 8 + target(row, col)[1])
        for row in range(16)
        for col in range(8)
    ]
    return lax.ppermute(block, AXES, pairs)


def to_column(row, col):
    y, z_lo, core = row >> 2, row >> 1 & 1, row & 1
    x, z_hi = col >> 1, col & 1
    return (x ^ 2 - core) * 4 + z_hi * 2 + core, y * 2 + z_lo


def join(*blocks):
    return jnp.concatenate(blocks, axis=0)


def body(record, taps, plan, quality):
    own = whiten(record, taps, plan, quality)
    both = join(own, send(own, lambda row, col: (row ^ 1, col)))
    other = send(own, lambda row, col: (row, col ^ S_MASKS[0]))
    receiver = send(both, to_column)
    other, _ = lax.optimization_barrier((other, both))
    source = join(own, other)
    source = join(source, send(source, lambda row, col: (row, col ^ S_MASKS[1])))
    receiver = join(
        receiver,
        send(receiver, lambda row, col: (row ^ (2 if row & 1 else 4), col)),
    )
    others = send(source, lambda row, col: (row, col ^ S_MASKS[2]))
    receiver = join(
        receiver,
        send(receiver, lambda row, col: (row ^ (4 if row & 1 else 2), col)),
    )
    rest = send(receiver, lambda row, col: (row ^ 1, col))
    return correlate(source, others, receiver, rest)


def solution(mesh):
    in_specs = (P(None, AXES, None), P(), P(), P(AXES))
    out_specs = P(None, "row", "col")
    return jax.shard_map(body, mesh=mesh, in_specs=in_specs, out_specs=out_specs, check_vma=False)
```

```python
import math

import jax
import jax.numpy as jnp
from jax import lax
from jax.experimental import pallas as pl
from jax.experimental.pallas import tpu as pltpu
from jax.sharding import PartitionSpec as P


STRIDE = 20
TAPS = 200
HALFWIN = 32
MAXLAG = 25
SUB = 4
LAGS = 51
FRAMES = 128
SEGMENT = 32 * STRIDE
SPAN = 896
AXES = ("row", "col")
GROUP = 3


def whiten_kernel(plan_ref, record_ref, taps_ref, quality_ref, out_ref, samples, sems):
    chans = out_ref.shape[0]
    f32, bf16 = jnp.float32, jnp.bfloat16
    raw = record_ref.shape[2]

    def copy(s):
        return pltpu.make_async_copy(
            record_ref.at[plan_ref[s]], samples.at[s, :, pl.ds(0, raw)], sems.at[s]
        )

    for s in range(SUB):
        copy(s).start()
    samples[:, :, raw:] = jnp.zeros((SUB, chans, samples.shape[2] - raw), bf16)
    taps = taps_ref[...].reshape(1, TAPS)
    table = jnp.broadcast_to(
        jnp.concatenate([taps, jnp.zeros((1, SPAN - TAPS), f32)], axis=1), (32, SPAN)
    )
    k = lax.broadcasted_iota(jnp.int32, (32, SPAN), 0)
    for bit in range(5):
        moved = pltpu.roll(table, STRIDE << bit, 1)
        table = jnp.where((k >> bit) & 1 == 1, moved, table)
    high = table.astype(bf16)
    low = (table - high.astype(f32)).astype(bf16)
    filters = jnp.concatenate([high] * 4 + [low] * 4, axis=0)
    i = lax.broadcasted_iota(jnp.int32, (2 * FRAMES, FRAMES), 0) & (FRAMES - 1)
    j = lax.broadcasted_iota(jnp.int32, (2 * FRAMES, FRAMES), 1)
    band = jnp.where(jnp.abs(i - j) <= HALFWIN, 1.0, 0.0).astype(bf16)
    a = lax.broadcasted_iota(jnp.int32, (chans, chans), 0)
    b = lax.broadcasted_iota(jnp.int32, (chans, chans), 1)
    across = jnp.broadcast_to(
        quality_ref[...].reshape(1, chans).astype(f32), (chans, chans)
    )
    quality = jnp.sum(jnp.where(a == b, across, 0.0), axis=1, keepdims=True)
    for s in range(SUB):
        copy(s).wait()
    both = lax.dot_general(
        jnp.concatenate(
            [
                samples[s, :, b * SEGMENT : b * SEGMENT + SPAN]
                for s in range(SUB)
                for b in range(4)
            ],
            axis=0,
        ),
        filters,
        (((1,), (1,)), ((), ())),
        preferred_element_type=f32,
    )
    both = both[:, :FRAMES] + both[:, FRAMES:]
    lane = lax.broadcasted_iota(jnp.int32, (chans, FRAMES), 1)
    rows = []
    for s in range(SUB):
        p = [both[(s * 4 + b) * chans : (s * 4 + b + 1) * chans] for b in range(4)]
        rows.append(
            jnp.where(
                lane < 64,
                jnp.where(lane < 32, p[0], p[1]),
                jnp.where(lane < 96, p[2], p[3]),
            )
        )
    decimated = jnp.concatenate(rows, axis=0)
    size = jnp.abs(decimated)
    size_high = size.astype(bf16)
    size_low = (size - size_high.astype(f32)).astype(bf16)
    envelope = jnp.dot(
        jnp.concatenate([size_high, size_low], axis=1), band, preferred_element_type=f32
    ) * (1.0 / (2 * HALFWIN + 1))
    for s in range(SUB):
        d = decimated[s * chans : (s + 1) * chans]
        e = envelope[s * chans : (s + 1) * chans]
        out_ref[:, s * FRAMES : (s + 1) * FRAMES] = (d / (e + 1e-05) * quality).astype(bf16)


def whiten(record, taps, plan, quality):
    chans, raw = record.shape[1:]
    return pl.pallas_call(
        whiten_kernel,
        name="whiten",
        out_shape=jax.ShapeDtypeStruct((chans, SUB * FRAMES), jnp.bfloat16),
        in_specs=[
            pl.BlockSpec(memory_space=pltpu.SMEM),
            pl.BlockSpec(memory_space=pltpu.HBM),
            pl.BlockSpec(memory_space=pltpu.VMEM),
            pl.BlockSpec(memory_space=pltpu.VMEM),
        ],
        out_specs=pl.BlockSpec(memory_space=pltpu.VMEM),
        scratch_shapes=[
            pltpu.VMEM((SUB, chans, raw + SPAN - SEGMENT), jnp.bfloat16),
            pltpu.SemaphoreType.DMA((SUB,)),
        ],
        compiler_params=pltpu.CompilerParams(vmem_limit_bytes=8 << 20),
        cost_estimate=pl.CostEstimate(flops=1 << 28, bytes_accessed=1 << 19, transcendentals=0),
    )(*(pltpu.with_memory_space_constraint(v, pltpu.HBM) for v in (plan, record, taps, quality)))


S_MASKS = (0, 2, 4, 6)


def spread(index, *masks):
    place = 0
    for bit, mask in enumerate(masks):
        if index >> bit & 1:
            place = place ^ mask
    return place


def correlate_kernel(*refs):
    s_refs, (r0_ref, r1_ref), (out_ref, source, receiver, products, sems) = (
        refs[:4],
        refs[4:6],
        refs[6:],
    )
    count, length = source.shape
    chans = count // 8
    col, row = lax.axis_index("col"), lax.axis_index("row")
    for part, mask in zip(s_refs, S_MASKS):
        for j in range(2):
            start = (col ^ mask ^ j) * chans
            source[pl.ds(pl.multiple_of(start, chans), chans)] = part[
                j * chans : (j + 1) * chans
            ].astype(jnp.float32)
    for half in range(2):
        core = (row & 1) ^ half
        part = (r0_ref, r1_ref)[half]
        for t in range(4):
            place = (row >> 1) ^ (4 - 2 * core) ^ spread(t, 2 - core, 1 + core)
            for j in range(2):
                start = ((core ^ j) * 8 + place) * chans
                receiver[pl.ds(pl.multiple_of(start, chans), chans)] = part[
                    (t * 2 + j) * chans : (t * 2 + j + 1) * chans
                ]
    turned = receiver[...].T
    lane = lax.broadcasted_iota(jnp.int32, (count, FRAMES), 1)
    scale = 1.0 / math.sqrt(length)

    def copy(g):
        part = pl.ds(g * GROUP, GROUP)
        return pltpu.make_async_copy(products.at[part], out_ref.at[part], sems.at[g])

    for g in range(LAGS // GROUP):
        moved = []
        for q in range(g * GROUP, (g + 1) * GROUP):
            shift = q - MAXLAG
            inside = (lane >= shift) & (lane < shift + FRAMES)
            moved.append(
                jnp.concatenate(
                    [
                        jnp.where(
                            inside,
                            pltpu.roll(
                                source[:, s * FRAMES : (s + 1) * FRAMES], shift % FRAMES, 1
                            ),
                            0.0,
                        ).astype(jnp.bfloat16)
                        for s in range(SUB)
                    ],
                    axis=1,
                )
            )
        product = jnp.dot(
            jnp.concatenate(moved, axis=0), turned, preferred_element_type=jnp.float32
        )
        products[g * GROUP : (g + 1) * GROUP] = (product * scale).reshape(GROUP, count, -1)
        copy(g).start()
    for g in range(LAGS // GROUP):
        copy(g).wait()


def correlate(*parts):
    count, width = 4 * parts[0].shape[0], 2 * parts[4].shape[0]
    length = parts[0].shape[1]
    whole = pl.BlockSpec(memory_space=pltpu.VMEM)
    return pl.pallas_call(
        correlate_kernel,
        name="correlate",
        out_shape=jax.ShapeDtypeStruct((LAGS, count, width), jnp.float32),
        in_specs=[whole] * 6,
        out_specs=pl.BlockSpec(memory_space=pl.ANY),
        scratch_shapes=[
            pltpu.VMEM((count, length), jnp.float32),
            pltpu.VMEM((width, length), jnp.bfloat16),
            pltpu.VMEM((LAGS, count, width), jnp.float32),
            pltpu.SemaphoreType.DMA((LAGS // GROUP,)),
        ],
        compiler_params=pltpu.CompilerParams(vmem_limit_bytes=24 << 20),
        cost_estimate=pl.CostEstimate(flops=1 << 31, bytes_accessed=1 << 23, transcendentals=0),
    )(*parts)


def send(block, target):
    pairs = [
        (row * 8 + col, target(row, col)[0] * 8 + target(row, col)[1])
        for row in range(16)
        for col in range(8)
    ]
    return lax.ppermute(block, AXES, pairs)


def to_column(row, col):
    y, z_lo, core = row >> 2, row >> 1 & 1, row & 1
    x, z_hi = col >> 1, col & 1
    return (x ^ 2 - core) * 4 + z_hi * 2 + core, y * 2 + z_lo


def join(*blocks):
    return jnp.concatenate(blocks, axis=0)


def body(record, taps, plan, quality):
    own = whiten(record, taps, plan, quality)
    both = join(own, send(own, lambda row, col: (row ^ 1, col)))
    other = send(own, lambda row, col: (row, col ^ 1))
    receiver = send(both, to_column)
    other, _ = lax.optimization_barrier((other, both))
    sources = [join(own, other)]
    for mask in S_MASKS[1:]:
        sources.append(send(sources[0], lambda row, col: (row, col ^ mask)))
    receiver = join(
        receiver,
        send(receiver, lambda row, col: (row ^ (2 if row & 1 else 4), col)),
    )
    receiver = join(
        receiver,
        send(receiver, lambda row, col: (row ^ (4 if row & 1 else 2), col)),
    )
    rest = send(receiver, lambda row, col: (row ^ 1, col))
    return correlate(*sources, receiver, rest)


def solution(mesh):
    in_specs = (P(None, AXES, None), P(), P(), P(AXES))
    out_specs = P(None, "row", "col")
    return jax.shard_map(body, mesh=mesh, in_specs=in_specs, out_specs=out_specs, check_vma=False)
```

```python
import math

import jax
import jax.numpy as jnp
from jax import lax
from jax.experimental import pallas as pl
from jax.experimental.pallas import tpu as pltpu
from jax.sharding import PartitionSpec as P


STRIDE = 20
TAPS = 200
HALFWIN = 32
MAXLAG = 25
SUB = 4
LAGS = 51
FRAMES = 128
SEGMENT = 32 * STRIDE
SPAN = 896
AXES = ("row", "col")
GROUP = 3


def whiten_kernel(
    plan_hbm, record_hbm, taps_hbm, quality_hbm, out_ref, plan, samples, taps_ref, quality_ref, sems
):
    chans = out_ref.shape[0]
    f32, bf16 = jnp.float32, jnp.bfloat16
    slots, _, raw = record_hbm.shape
    copies = [
        pltpu.make_async_copy(plan_hbm, plan, sems.at[0]),
        pltpu.make_async_copy(taps_hbm, taps_ref, sems.at[1]),
        pltpu.make_async_copy(quality_hbm, quality_ref, sems.at[2]),
    ] + [
        pltpu.make_async_copy(record_hbm.at[s], samples.at[s, :, pl.ds(0, raw)], sems.at[3 + s])
        for s in range(slots)
    ]
    for copy in copies:
        copy.start()
    samples[:, :, raw:] = jnp.zeros((slots, chans, samples.shape[2] - raw), bf16)
    copies[1].wait()
    taps = taps_ref[...].reshape(1, TAPS)
    table = jnp.broadcast_to(
        jnp.concatenate([taps, jnp.zeros((1, SPAN - TAPS), f32)], axis=1), (32, SPAN)
    )
    k = lax.broadcasted_iota(jnp.int32, (32, SPAN), 0)
    for bit in range(5):
        moved = pltpu.roll(table, STRIDE << bit, 1)
        table = jnp.where((k >> bit) & 1 == 1, moved, table)
    high = table.astype(bf16)
    low = (table - high.astype(f32)).astype(bf16)
    filters = jnp.concatenate([high] * 4 + [low] * 4, axis=0)
    i = lax.broadcasted_iota(jnp.int32, (2 * FRAMES, FRAMES), 0) & (FRAMES - 1)
    j = lax.broadcasted_iota(jnp.int32, (2 * FRAMES, FRAMES), 1)
    band = jnp.where(jnp.abs(i - j) <= HALFWIN, 1.0, 0.0).astype(bf16)
    a = lax.broadcasted_iota(jnp.int32, (chans, chans), 0)
    b = lax.broadcasted_iota(jnp.int32, (chans, chans), 1)
    copies[2].wait()
    across = jnp.broadcast_to(
        quality_ref[...].reshape(1, chans).astype(f32), (chans, chans)
    )
    quality = jnp.sum(jnp.where(a == b, across, 0.0), axis=1, keepdims=True)
    for copy in copies[:1] + copies[3:]:
        copy.wait()
    both = lax.dot_general(
        jnp.concatenate(
            [
                samples[plan[s], :, b * SEGMENT : b * SEGMENT + SPAN]
                for s in range(SUB)
                for b in range(4)
            ],
            axis=0,
        ),
        filters,
        (((1,), (1,)), ((), ())),
        preferred_element_type=f32,
    )
    both = both[:, :FRAMES] + both[:, FRAMES:]
    lane = lax.broadcasted_iota(jnp.int32, (chans, FRAMES), 1)
    rows = []
    for s in range(SUB):
        p = [both[(s * 4 + b) * chans : (s * 4 + b + 1) * chans] for b in range(4)]
        rows.append(
            jnp.where(
                lane < 64,
                jnp.where(lane < 32, p[0], p[1]),
                jnp.where(lane < 96, p[2], p[3]),
            )
        )
    decimated = jnp.concatenate(rows, axis=0)
    size = jnp.abs(decimated)
    size_high = size.astype(bf16)
    size_low = (size - size_high.astype(f32)).astype(bf16)
    envelope = jnp.dot(
        jnp.concatenate([size_high, size_low], axis=1), band, preferred_element_type=f32
    ) * (1.0 / (2 * HALFWIN + 1))
    for s in range(SUB):
        d = decimated[s * chans : (s + 1) * chans]
        e = envelope[s * chans : (s + 1) * chans]
        out_ref[:, s * FRAMES : (s + 1) * FRAMES] = (d / (e + 1e-05) * quality).astype(bf16)


def whiten(record, taps, plan, quality):
    chans, raw = record.shape[1:]
    return pl.pallas_call(
        whiten_kernel,
        name="whiten",
        out_shape=jax.ShapeDtypeStruct((chans, SUB * FRAMES), jnp.bfloat16),
        in_specs=[pl.BlockSpec(memory_space=pltpu.HBM)] * 4,
        out_specs=pl.BlockSpec(memory_space=pltpu.VMEM),
        scratch_shapes=[
            pltpu.SMEM(plan.shape, jnp.int32),
            pltpu.VMEM((record.shape[0], chans, raw + SPAN - SEGMENT), jnp.bfloat16),
            pltpu.VMEM(taps.shape, jnp.float32),
            pltpu.VMEM(quality.shape, jnp.int32),
            pltpu.SemaphoreType.DMA((3 + record.shape[0],)),
        ],
        compiler_params=pltpu.CompilerParams(vmem_limit_bytes=8 << 20),
        cost_estimate=pl.CostEstimate(flops=1 << 28, bytes_accessed=1 << 19, transcendentals=0),
    )(*(pltpu.with_memory_space_constraint(v, pltpu.HBM) for v in (plan, record, taps, quality)))


S_MASKS = (0, 2, 4, 6)


def spread(index, *masks):
    place = 0
    for bit, mask in enumerate(masks):
        if index >> bit & 1:
            place = place ^ mask
    return place


def correlate_kernel(*refs):
    s_refs, (r0_ref, r1_ref), (out_ref, source, receiver, products, sems) = (
        refs[:4],
        refs[4:6],
        refs[6:],
    )
    count, length = source.shape
    chans = count // 8
    col, row = lax.axis_index("col"), lax.axis_index("row")
    for part, mask in zip(s_refs, S_MASKS):
        for j in range(2):
            start = (col ^ mask ^ j) * chans
            source[pl.ds(pl.multiple_of(start, chans), chans)] = part[
                j * chans : (j + 1) * chans
            ].astype(jnp.float32)
    for half in range(2):
        core = (row & 1) ^ half
        part = (r0_ref, r1_ref)[half]
        for t in range(4):
            place = (row >> 1) ^ (4 - 2 * core) ^ spread(t, 2 - core, 1 + core)
            for j in range(2):
                start = ((core ^ j) * 8 + place) * chans
                receiver[pl.ds(pl.multiple_of(start, chans), chans)] = part[
                    (t * 2 + j) * chans : (t * 2 + j + 1) * chans
                ]
    turned = receiver[...].T
    lane = lax.broadcasted_iota(jnp.int32, (count, FRAMES), 1)
    scale = 1.0 / math.sqrt(length)

    def copy(g):
        part = pl.ds(g * GROUP, GROUP)
        return pltpu.make_async_copy(products.at[part], out_ref.at[part], sems.at[g])

    for g in range(LAGS // GROUP):
        moved = []
        for q in range(g * GROUP, (g + 1) * GROUP):
            shift = q - MAXLAG
            inside = (lane >= shift) & (lane < shift + FRAMES)
            moved.append(
                jnp.concatenate(
                    [
                        jnp.where(
                            inside,
                            pltpu.roll(
                                source[:, s * FRAMES : (s + 1) * FRAMES], shift % FRAMES, 1
                            ),
                            0.0,
                        ).astype(jnp.bfloat16)
                        for s in range(SUB)
                    ],
                    axis=1,
                )
            )
        product = jnp.dot(
            jnp.concatenate(moved, axis=0), turned, preferred_element_type=jnp.float32
        )
        products[g * GROUP : (g + 1) * GROUP] = (product * scale).reshape(GROUP, count, -1)
        copy(g).start()
    for g in range(LAGS // GROUP):
        copy(g).wait()


def correlate(*parts):
    count, width = 4 * parts[0].shape[0], 2 * parts[4].shape[0]
    length = parts[0].shape[1]
    whole = pl.BlockSpec(memory_space=pltpu.VMEM)
    return pl.pallas_call(
        correlate_kernel,
        name="correlate",
        out_shape=jax.ShapeDtypeStruct((LAGS, count, width), jnp.float32),
        in_specs=[whole] * 6,
        out_specs=pl.BlockSpec(memory_space=pl.ANY),
        scratch_shapes=[
            pltpu.VMEM((count, length), jnp.float32),
            pltpu.VMEM((width, length), jnp.bfloat16),
            pltpu.VMEM((LAGS, count, width), jnp.float32),
            pltpu.SemaphoreType.DMA((LAGS // GROUP,)),
        ],
        compiler_params=pltpu.CompilerParams(vmem_limit_bytes=24 << 20),
        cost_estimate=pl.CostEstimate(flops=1 << 31, bytes_accessed=1 << 23, transcendentals=0),
    )(*parts)


def send(block, target):
    pairs = [
        (row * 8 + col, target(row, col)[0] * 8 + target(row, col)[1])
        for row in range(16)
        for col in range(8)
    ]
    return lax.ppermute(block, AXES, pairs)


def to_column(row, col):
    y, z_lo, core = row >> 2, row >> 1 & 1, row & 1
    x, z_hi = col >> 1, col & 1
    return (x ^ 2 - core) * 4 + z_hi * 2 + core, y * 2 + z_lo


def join(*blocks):
    return jnp.concatenate(blocks, axis=0)


def body(record, taps, plan, quality):
    own = whiten(record, taps, plan, quality)
    both = join(own, send(own, lambda row, col: (row ^ 1, col)))
    other = send(own, lambda row, col: (row, col ^ 1))
    receiver = send(both, to_column)
    other, _ = lax.optimization_barrier((other, both))
    sources = [join(own, other)]
    for mask in S_MASKS[1:]:
        sources.append(send(sources[0], lambda row, col: (row, col ^ mask)))
    receiver = join(
        receiver,
        send(receiver, lambda row, col: (row ^ (2 if row & 1 else 4), col)),
    )
    receiver = join(
        receiver,
        send(receiver, lambda row, col: (row ^ (4 if row & 1 else 2), col)),
    )
    rest = send(receiver, lambda row, col: (row ^ 1, col))
    return correlate(*sources, receiver, rest)


def solution(mesh):
    in_specs = (P(None, AXES, None), P(), P(), P(AXES))
    out_specs = P(None, "row", "col")
    return jax.shard_map(body, mesh=mesh, in_specs=in_specs, out_specs=out_specs, check_vma=False)
```
